32 devices in a mesh: blk: 8 (over z, x), grp: 4 (over y, core).
Axes of the slice: x: 2, y: 2, z: 4, core: 2. Of those that a mesh axis runs over, the one named last changes fastest.
Arguments:
- row_factors: float32 [65536, 256], P(('blk', 'grp')), may hold values from -1.5 to 1.5
- row_accum: float32 [65536], P(('blk', 'grp')), may hold values from 1 to 100
- col_factors: float32 [8192, 256], P('blk'), may hold values from -1.5 to 1.5
- col_accum: float32 [8192], P('blk'), may hold values from 1 to 100
- tile_values: bfloat16 [32, 3, 32, 128, 128], P(('blk', 'grp')), may hold values from -6 to 6
- tile_rows: int32 [32, 3, 32], P(('blk', 'grp')), may hold values from 0 to 15, as said below
- tile_cols: int32 [32, 3, 32], P(('blk', 'grp')), may hold values from 0 to 7
Outputs:
- new_row_factors: float32 [65536, 256], P(('blk', 'grp'))
- new_row_accum: float32 [65536], P(('blk', 'grp'))
- new_col_factors: float32 [8192, 256], P('blk')
- new_col_accum: float32 [8192], P('blk')
The draws below stay inside these ranges and needn't reach their ends.
Inputs may be any that keep to these rules, and one draw needn't show every extreme that they name: For each strip and step, tile_rows and tile_cols together name 32 different tiles.
All inputs are finite; a program needn't handle non-finite values.
Results may differ from the reference program's by a relative error of at most 0.004.
Values may be sent and summed in bfloat16 or wider, within the bound.
No kernel may reach another device: no remote copies, remote signals or barrier semaphores. Data moves between devices by JAX's collectives and lax.ppermute only.
A program may use at most 64 MiB of HBM per device.

```python
import math
import jax
import jax.numpy as jnp
from jax import lax

K = 256
CB = 1024
TILE = 128
ROWS_DEV = 2048
STEPS = 3
FILLED = 32
STRIPS = 32
ROWS = 65536
COLS = 8192
N_BLK = 8
N_GRP = 4


def tile_pairs(key):
    key_list = jax.random.split(jax.random.fold_in(key, 31), STRIPS * STEPS)

    def pick_tiles(single_key):
        return jax.random.permutation(single_key, ROWS_DEV // TILE * (CB // TILE))[:FILLED]
    tile_picks = jax.vmap(pick_tiles)(key_list)
    return tile_picks.reshape(STRIPS, STEPS, FILLED).astype(jnp.int32)


def draw_tile_rows(key, part):
    return tile_pairs(key) // (CB // TILE)


def draw_tile_cols(key, part):
    return tile_pairs(key) % (CB // TILE)


def shard_levels(stream_key, extent, cuts, least, high):
    gain = 1.0
    for position, blocks in cuts:
        draws = jax.random.uniform(jax.random.fold_in(jax.random.fold_in(stream_key, 6), position), (blocks,), jnp.float32, least / len(cuts), high / len(cuts))
        gain = gain * jnp.repeat(jnp.exp(draws), extent[position] // blocks).reshape((-1,) + (1,) * (len(extent) - 1 - position))
    return gain


def gaussian(own_key, extent, deviation, most, cuts=(), held_as=jnp.bfloat16):
    level = shard_levels(own_key, extent, cuts, -0.22, 0.18) if cuts else 1.0
    entries = jax.random.normal(own_key, extent, jnp.float32) * deviation * level
    return jnp.minimum(jnp.maximum(entries, -most), most).astype(held_as)


def setup_inputs(seed: int = 0) -> dict:
    splits = jax.random.split(jax.random.key(seed), 8)
    return {
        "row_factors": gaussian(splits[0], (ROWS, K), 0.25, 1.5, ((0, 32),), jnp.float32),
        "row_accum": jnp.clip(jnp.exp(math.log(100.0) - 4.6051702 * jax.random.uniform(splits[1], (ROWS,), jnp.float32) ** shard_levels(splits[1], (ROWS,), ((0, 32),), -0.2, 0.2)), 1.0, 100.0),
        "col_factors": gaussian(splits[2], (COLS, K), 0.25, 1.5, ((0, 8),), jnp.float32),
        "col_accum": jnp.clip(jnp.exp(math.log(100.0) - 4.6051702 * jax.random.uniform(splits[3], (COLS,), jnp.float32) ** shard_levels(splits[3], (COLS,), ((0, 8),), -0.2, 0.2)), 1.0, 100.0),
        "tile_values": gaussian(splits[4], (STRIPS, STEPS, FILLED, TILE, TILE), 1.0, 6.0, ((0, 32),)),
        "tile_rows": draw_tile_rows(jax.random.fold_in(splits[7], 71), 0),
        "tile_cols": draw_tile_cols(jax.random.fold_in(splits[7], 71), 0),
    }


learn_rate = 0.1

def adagrad_rows(weights, accum, grads):
    accum_new = accum + lax.optimization_barrier(jnp.mean(grads * grads, axis=-1))
    return (weights - learn_rate * grads / jnp.sqrt(accum_new)[..., None], accum_new)

def rounded(matrix):
    return lax.optimization_barrier(matrix.astype(jnp.bfloat16)).astype(jnp.float32)

def strip_grads(strip_rows, block_cols, values, row_index, col_index):
    row_tiles = rounded(strip_rows).reshape(ROWS_DEV // TILE, TILE, K)
    col_tiles = rounded(block_cols).reshape(CB // TILE, TILE, K)
    left_tiles = row_tiles[row_index]
    right_tiles = col_tiles[col_index]
    predicted = jnp.einsum('fik,fjk->fij', left_tiles, right_tiles, precision=lax.Precision.HIGHEST)
    errors = rounded(predicted - values.astype(jnp.float32))
    row_grads = jnp.einsum('fij,fjk->fik', errors, right_tiles, precision=lax.Precision.HIGHEST)
    col_grads = jnp.einsum('fij,fik->fjk', errors, left_tiles, precision=lax.Precision.HIGHEST)
    row_sum = jax.ops.segment_sum(row_grads, row_index, num_segments=ROWS_DEV // TILE).reshape(ROWS_DEV, K)
    col_sum = jax.ops.segment_sum(col_grads, col_index, num_segments=CB // TILE).reshape(CB, K)
    return (row_sum, col_sum)

def one_block(packed):
    strips, block_cols, block_values, block_rows, block_colidx = packed
    return jax.vmap(strip_grads, in_axes=(0, None, 0, 0, 0))(strips, block_cols, block_values, block_rows, block_colidx)

def reference(row_factors, row_accum, col_factors, col_accum, tile_values, tile_rows, tile_cols):
    row_state = row_factors.reshape(N_BLK, N_GRP, ROWS_DEV, K)
    row_acc = row_accum.reshape(N_BLK, N_GRP, ROWS_DEV)
    col_blocks = col_factors.reshape(N_BLK, CB, K)
    col_acc = col_accum.reshape(N_BLK, CB)
    values = tile_values.reshape(N_BLK, N_GRP, STEPS, FILLED, TILE, TILE)
    row_lists = tile_rows.reshape(N_BLK, N_GRP, STEPS, FILLED)
    col_lists = tile_cols.reshape(N_BLK, N_GRP, STEPS, FILLED)
    for rotation in range(STEPS):
        current = jnp.roll(col_blocks, -rotation, axis=0)
        current_acc = jnp.roll(col_acc, -rotation, axis=0)
        row_grads, col_grads = lax.map(one_block, (row_state, current, values[:, :, rotation], row_lists[:, :, rotation], col_lists[:, :, rotation]))
        row_state, row_acc = adagrad_rows(row_state, row_acc, row_grads)
        current, current_acc = adagrad_rows(current, current_acc, lax.optimization_barrier(jnp.sum(col_grads, axis=1)))
        col_blocks = jnp.roll(current, rotation, axis=0)
        col_acc = jnp.roll(current_acc, rotation, axis=0)
    return (row_state.reshape(ROWS, K), row_acc.reshape(ROWS), col_blocks.reshape(COLS, K), col_acc.reshape(COLS))
```

```python
import functools

import jax
import jax.numpy as jnp
from jax import lax
from jax.experimental import pallas as pl
from jax.experimental.pallas import tpu as pltpu
from jax.sharding import PartitionSpec as P

LEARN_RATE = 0.1
F32 = jnp.float32
BF16 = jnp.bfloat16
VMEM = pl.BlockSpec(memory_space=pltpu.VMEM)
SMEM = pl.BlockSpec(memory_space=pltpu.SMEM)
ANY = pl.BlockSpec(memory_space=pl.ANY)
GRANT = 24 * 1024 * 1024


def call(body, out_shape, in_specs, scratch, flops, moved):
    return pl.pallas_call(
        body,
        out_shape=out_shape,
        in_specs=in_specs,
        out_specs=jax.tree.map(lambda _: VMEM, out_shape),
        scratch_shapes=scratch,
        compiler_params=pltpu.CompilerParams(vmem_limit_bytes=GRANT),
        cost_estimate=pl.CostEstimate(flops=flops, bytes_accessed=moved, transcendentals=0),
    )


def shape(dims, dtype):
    return jax.ShapeDtypeStruct(dims, dtype)


def dot(left, right, dims):
    return lax.dot_general(left, right, (dims, ((), ())), preferred_element_type=F32)


def place_halves(side_ref, own_ref, sib_ref, joined):
    tiles, tile, _ = joined.shape
    part = tiles // 2
    side = side_ref[0]
    for j in range(part):
        joined[side * part + j] = own_ref[j * tile : (j + 1) * tile, :].astype(BF16)
        joined[(1 - side) * part + j] = sib_ref[j * tile : (j + 1) * tile, :].astype(BF16)


def col_body(
    step, chunks, side_ref, tr_ref, tc_ref, rows_ref, own_ref, sib_ref, tv_ref,
    keep_ref, send_ref, err_ref, vis, acc, vals, rows_b, sems,
):
    filled, tile, _ = vals.shape
    per = filled // chunks
    copies = [
        pltpu.make_async_copy(
            tv_ref.at[0, step, pl.ds(j * per, per)], vals.at[pl.ds(j * per, per)], sems.at[j]
        )
        for j in range(chunks)
    ]
    for copy in copies:
        copy.start()
    place_halves(side_ref, own_ref, sib_ref, vis)
    acc[...] = jnp.zeros_like(acc)
    for r in range(rows_b.shape[0]):
        rows_b[r] = rows_ref[r * tile : (r + 1) * tile, :].astype(BF16)

    def one(f, carry):
        r = tr_ref[step, f]
        c = tc_ref[step, f]
        left = rows_b[r]
        predicted = dot(left, vis[c], ((1,), (1,)))
        errors = (predicted - vals[f].astype(F32)).astype(BF16)
        err_ref[f] = errors
        acc[c] += dot(errors, left, ((0,), (0,)))
        return carry

    for j in range(chunks):
        copies[j].wait()
        lax.fori_loop(j * per, (j + 1) * per, one, 0, unroll=4)
    part = vis.shape[0] // 2
    side = side_ref[0]
    for j in range(part):
        keep_ref[j * tile : (j + 1) * tile, :] = acc[side * part + j]
        send_ref[j * tile : (j + 1) * tile, :] = acc[(1 - side) * part + j].astype(BF16)


def adagrad(weights, accum_row, grads):
    tile, width = grads.shape
    eye = lax.broadcasted_iota(jnp.int32, (tile, tile), 0) == lax.broadcasted_iota(
        jnp.int32, (tile, tile), 1
    )
    mean = jnp.sum(grads * grads, axis=1, keepdims=True) * (1.0 / width)
    new_row = accum_row + jnp.sum(jnp.where(eye, mean, 0.0), axis=0, keepdims=True)
    new_col = jnp.sum(jnp.where(eye, new_row, 0.0), axis=1, keepdims=True)
    return weights - grads * (LEARN_RATE / jnp.sqrt(new_col)), new_row


def row_body(
    step, side_ref, tr_ref, tc_ref, err_ref, own_ref, sib_ref, rows_ref, accum_ref,
    new_ref, new_accum_ref, new_b_ref, vis, acc,
):
    filled, tile, _ = err_ref.shape
    place_halves(side_ref, own_ref, sib_ref, vis)
    acc[...] = jnp.zeros_like(acc)

    def one(f, carry):
        acc[tr_ref[step, f]] += dot(err_ref[f], vis[tc_ref[step, f]], ((1,), (0,)))
        return carry

    lax.fori_loop(0, filled, one, 0, unroll=4)

    def update(r, carry):
        span = pl.ds(pl.multiple_of(r * tile, tile), tile)
        new, new_row = adagrad(rows_ref[span, :], accum_ref[pl.ds(r, 1), :], acc[r])
        new_ref[span, :] = new
        new_b_ref[span, :] = new.astype(BF16)
        new_accum_ref[pl.ds(r, 1), :] = new_row
        return carry

    lax.fori_loop(0, acc.shape[0], update, 0)


def split_update(tile, states, accum_ref, grads, out):
    for j in range(accum_ref.shape[0]):
        span = slice(j * tile, (j + 1) * tile)
        weights = states[0][span, :].astype(F32)
        for other in states[1:]:
            weights = weights + other[span, :].astype(F32)
        total = grads[0][span, :].astype(F32)
        for other in grads[1:]:
            total = total + other[span, :].astype(F32)
        new, new_row = adagrad(weights, accum_ref[j : j + 1, :], total)
        out(span, j, new, new_row, total)


def first_update_body(n_grad, *refs):
    state_ref, accum_ref = refs[:2]
    grads = refs[2 : 2 + n_grad]
    high_ref, low_ref, new_ref, new_accum_ref = refs[2 + n_grad :]
    tile = accum_ref.shape[1]

    def out(span, j, new, new_row, total):
        high = new.astype(BF16)
        high_ref[span, :] = high
        low_ref[span, :] = (new - high.astype(F32)).astype(BF16)
        new_ref[span, :] = new
        new_accum_ref[j : j + 1, :] = new_row

    split_update(tile, (state_ref,), accum_ref, grads, out)


def next_update_body(n_grad, *refs):
    high_in, low_in, accum_ref = refs[:3]
    grads = refs[3 : 3 + n_grad]
    high_ref, low_ref, new_accum_ref, total_ref = refs[3 + n_grad :]
    tile = accum_ref.shape[1]

    def out(span, j, new, new_row, total):
        high = new.astype(BF16)
        high_ref[span, :] = high
        low_ref[span, :] = (new - high.astype(F32)).astype(BF16)
        new_accum_ref[j : j + 1, :] = new_row
        total_ref[span, :] = total.astype(BF16)

    split_update(tile, (high_in, low_in), accum_ref, grads, out)


def home_update_body(n_grad, *refs):
    state_ref, accum_ref = refs[:2]
    grads = refs[2 : 2 + n_grad]
    new_ref, new_accum_ref = refs[2 + n_grad :]
    tile = accum_ref.shape[1]

    def out(span, j, new, new_row, total):
        new_ref[span, :] = new
        new_accum_ref[j : j + 1, :] = new_row

    split_update(tile, (state_ref,), accum_ref, grads, out)


def shifted(value, by):
    count = lax.axis_size("blk")
    return lax.ppermute(value, "blk", [(i, (i + by) % count) for i in range(count)])


def sibling(value):
    return lax.ppermute(value, "grp", [(i, i ^ 1) for i in range(lax.axis_size("grp"))])


def across(value):
    count = lax.axis_size("grp")
    return [
        lax.ppermute(value, "grp", [(i, (i + by) % count) for i in range(count)])
        for by in range(2, count, 2)
    ]


def local(row_factors, row_accum, col_factors, col_accum, tile_values, tile_rows, tile_cols):
    strip_len, width = row_factors.shape
    block_len = col_factors.shape[0]
    _, steps, filled, tile, _ = tile_values.shape
    row_tiles, col_tiles = strip_len // tile, block_len // tile
    half, part = block_len // 2, col_tiles // 2
    side = lax.rem(lax.axis_index("grp"), 2)
    side_arg = jnp.full((1,), side, jnp.int32)
    tr, tc = tile_rows[0], tile_cols[0]
    n_grad = lax.axis_size("grp") // 2
    chunks = 4 if filled % 4 == 0 else 1

    own = lax.dynamic_slice_in_dim(col_factors, side * half, half, 0)
    sib = lax.dynamic_slice_in_dim(col_factors, (1 - side) * half, half, 0)
    accum2 = col_accum.reshape(col_tiles, tile)
    own_accum = lax.dynamic_slice_in_dim(accum2, side * part, part, 0)
    state, factors, factors_b = own, row_factors, row_factors
    low = None
    factor_acc = row_accum.reshape(row_tiles, tile)
    home = home_accum = None
    pair_flops = 2 * filled * tile * tile * width
    half_f, half_b = shape((half, width), F32), shape((half, width), BF16)
    accum_s = shape((part, tile), F32)

    for step in range(steps):
        keep, send, errors = call(
            functools.partial(col_body, step, chunks),
            (half_f, half_b, shape((filled, tile, tile), BF16)),
            [SMEM, SMEM, SMEM, VMEM, VMEM, VMEM, ANY],
            [
                pltpu.VMEM((col_tiles, tile, width), BF16),
                pltpu.VMEM((col_tiles, tile, width), F32),
                pltpu.VMEM((filled, tile, tile), BF16),
                pltpu.VMEM((row_tiles, tile, width), BF16),
                pltpu.SemaphoreType.DMA((chunks,)),
            ],
            2 * pair_flops,
            4 * filled * tile * tile,
        )(side_arg, tr, tc, factors_b, own, sib, tile_values)
        chip_sum = (keep + sibling(send).astype(F32)).astype(BF16)
        if step == steps - 1:
            chip_sum = shifted(chip_sum, steps - 1)
        grads = [chip_sum] + across(chip_sum)
        factors, factor_acc, factors_b = call(
            functools.partial(row_body, step),
            (
                shape((strip_len, width), F32),
                shape((row_tiles, tile), F32),
                shape((strip_len, width), BF16),
            ),
            [SMEM, SMEM, SMEM, VMEM, VMEM, VMEM, VMEM, VMEM],
            [
                pltpu.VMEM((col_tiles, tile, width), BF16),
                pltpu.VMEM((row_tiles, tile, width), F32),
            ],
            pair_flops,
            10 * strip_len * width,
        )(side_arg, tr, tc, errors, own, sib, factors, factor_acc)
        if step == steps - 1:
            break
        if step == 0:
            high, low, home, home_accum = call(
                functools.partial(first_update_body, n_grad),
                (half_b, half_b, half_f, accum_s),
                [VMEM] * (2 + n_grad), [], 8 * half * width, 8 * half * width,
            )(state, own_accum, *grads)
            own_accum = home_accum
        else:
            high, low, own_accum, total = call(
                functools.partial(next_update_body, n_grad),
                (half_b, half_b, accum_s, half_b),
                [VMEM] * (3 + n_grad), [], 8 * half * width, 8 * half * width,
            )(own, low, own_accum, *grads)
        own = shifted(high, -1)
        low = shifted(low, -1)
        own_accum = shifted(own_accum, -1)
        sib = sibling(own)
        if step > 0:
            home, home_accum = call(
                functools.partial(home_update_body, 1),
                (half_f, accum_s), [VMEM] * 3, [], 8 * half * width, 8 * half * width,
            )(home, home_accum, shifted(total, step))

    if steps == 1:
        home, home_accum = state, own_accum
    new, new_accum = call(
        functools.partial(home_update_body, n_grad),
        (half_f, accum_s), [VMEM] * (2 + n_grad), [], 8 * half * width, 8 * half * width,
    )(home, home_accum, *grads)
    new_s, new_accum_s = sibling(new), sibling(new_accum)
    first = side == 0

    def joined(mine, other):
        return jnp.concatenate([jnp.where(first, mine, other), jnp.where(first, other, mine)])

    return (
        factors,
        factor_acc.reshape(strip_len),
        joined(new, new_s),
        joined(new_accum, new_accum_s).reshape(block_len),
    )


def solution(mesh):
    placed = (
        P(("blk", "grp"), None),
        P(("blk", "grp")),
        P("blk", None),
        P("blk"),
        P(("blk", "grp"), None, None, None, None),
        P(("blk", "grp"), None, None),
        P(("blk", "grp"), None, None),
    )
    return jax.shard_map(
        local,
        mesh=mesh,
        in_specs=placed,
        out_specs=(P(("blk", "grp"), None), P(("blk", "grp")), P("blk", None), P("blk")),
        check_vma=False,
    )
```

```python
import functools

import jax
import jax.numpy as jnp
from jax import lax
from jax.experimental import pallas as pl
from jax.experimental.pallas import tpu as pltpu
from jax.sharding import PartitionSpec as P

LEARN_RATE = 0.1
F32 = jnp.float32
BF16 = jnp.bfloat16
VMEM = pl.BlockSpec(memory_space=pltpu.VMEM)
SMEM = pl.BlockSpec(memory_space=pltpu.SMEM)
ANY = pl.BlockSpec(memory_space=pl.ANY)
HBM = pl.BlockSpec(memory_space=pltpu.HBM)
GRANT = 12 * 1024 * 1024


def call(body, out_shape, in_specs, scratch, flops, moved):
    return pl.pallas_call(
        body,
        out_shape=out_shape,
        in_specs=in_specs,
        out_specs=jax.tree.map(lambda _: VMEM, out_shape),
        scratch_shapes=scratch,
        compiler_params=pltpu.CompilerParams(vmem_limit_bytes=GRANT),
        cost_estimate=pl.CostEstimate(flops=flops, bytes_accessed=moved, transcendentals=0),
    )


def shape(dims, dtype):
    return jax.ShapeDtypeStruct(dims, dtype)


def dot(left, right, dims):
    return lax.dot_general(left, right, (dims, ((), ())), preferred_element_type=F32)


def place_halves(side_ref, own_ref, sib_ref, joined):
    tiles, tile, _ = joined.shape
    if own_ref.shape[0] == tiles * tile:
        for j in range(tiles):
            joined[j] = own_ref[j * tile : (j + 1) * tile, :].astype(BF16)
        return
    part = tiles // 2
    side = side_ref[0]
    for j in range(part):
        joined[side * part + j] = own_ref[j * tile : (j + 1) * tile, :].astype(BF16)
        joined[(1 - side) * part + j] = sib_ref[j * tile : (j + 1) * tile, :].astype(BF16)


def col_body(
    step, chunks, side_ref, tr_ref, tc_ref, rows_ref, own_ref, sib_ref, tv_ref,
    keep_ref, send_ref, err_ref, vis, acc, vals, rows_b, sems,
):
    filled, tile, _ = vals.shape
    per = filled // chunks
    copies = [
        pltpu.make_async_copy(
            tv_ref.at[0, step, pl.ds(j * per, per)], vals.at[pl.ds(j * per, per)], sems.at[j]
        )
        for j in range(chunks)
    ]
    for copy in copies:
        copy.start()
    place_halves(side_ref, own_ref, sib_ref, vis)
    acc[...] = jnp.zeros_like(acc)
    for r in range(rows_b.shape[0]):
        rows_b[r] = rows_ref[r * tile : (r + 1) * tile, :].astype(BF16)

    def one(f, carry):
        r = tr_ref[step, f]
        c = tc_ref[step, f]
        left = rows_b[r]
        predicted = dot(left, vis[c], ((1,), (1,)))
        errors = (predicted - vals[f].astype(F32)).astype(BF16)
        err_ref[f] = errors
        acc[c] += dot(errors, left, ((0,), (0,)))
        return carry

    for j in range(chunks):
        copies[j].wait()
        lax.fori_loop(j * per, (j + 1) * per, one, 0, unroll=4)
    part = vis.shape[0] // 2
    side = side_ref[0]
    for j in range(part):
        keep_ref[j * tile : (j + 1) * tile, :] = acc[side * part + j]
        send_ref[j * tile : (j + 1) * tile, :] = acc[(1 - side) * part + j].astype(BF16)


def adagrad(weights, accum_row, grads):
    tile, width = grads.shape
    eye = lax.broadcasted_iota(jnp.int32, (tile, tile), 0) == lax.broadcasted_iota(
        jnp.int32, (tile, tile), 1
    )
    mean = jnp.sum(grads * grads, axis=1, keepdims=True) * (1.0 / width)
    new_row = accum_row + jnp.sum(jnp.where(eye, mean, 0.0), axis=0, keepdims=True)
    new_col = jnp.sum(jnp.where(eye, new_row, 0.0), axis=1, keepdims=True)
    return weights - grads * (LEARN_RATE / jnp.sqrt(new_col)), new_row


def row_body(
    step, side_ref, tr_ref, tc_ref, err_ref, own_ref, sib_ref, rows_ref, accum_ref, _,
    new_ref, new_accum_ref, new_b_ref, vis, acc,
):
    filled, tile, _ = err_ref.shape
    place_halves(side_ref, own_ref, sib_ref, vis)
    acc[...] = jnp.zeros_like(acc)

    def one(f, carry):
        acc[tr_ref[step, f]] += dot(err_ref[f], vis[tc_ref[step, f]], ((1,), (0,)))
        return carry

    lax.fori_loop(0, filled, one, 0, unroll=4)

    def update(r, carry):
        span = pl.ds(pl.multiple_of(r * tile, tile), tile)
        new, new_row = adagrad(rows_ref[span, :], accum_ref[pl.ds(r, 1), :], acc[r])
        new_ref[span, :] = new
        new_b_ref[span, :] = new.astype(BF16)
        new_accum_ref[pl.ds(r, 1), :] = new_row
        return carry

    lax.fori_loop(0, acc.shape[0], update, 0)


def split_update(tile, count, weights_of, accum_of, grads_of, out):
    for j in range(count):
        span = slice(j * tile, (j + 1) * tile)
        total = functools.reduce(jnp.add, [g[span, :].astype(F32) for g in grads_of])
        new, new_row = adagrad(weights_of(j, span), accum_of(j), total)
        out(span, j, new, new_row, total)


def first_update_body(n_grad, side_ref, _, cols_ref, accum_ref, *refs):
    grads = refs[:n_grad]
    high_ref, low_ref, new_ref, new_accum_ref = refs[n_grad:]
    part, tile = new_accum_ref.shape
    side = side_ref[0]

    def weights_of(j, span):
        return cols_ref[pl.ds(pl.multiple_of((side * part + j) * tile, tile), tile), :]

    def out(span, j, new, new_row, total):
        high = new.astype(BF16)
        high_ref[span, :] = high
        low_ref[span, :] = (new - high.astype(F32)).astype(BF16)
        new_ref[span, :] = new
        new_accum_ref[j : j + 1, :] = new_row

    split_update(
        tile, part, weights_of, lambda j: accum_ref[pl.ds(side * part + j, 1), :], grads, out
    )


def next_update_body(n_grad, _, high_in, low_in, accum_ref, *refs):
    grads = refs[:n_grad]
    high_ref, low_ref, new_accum_ref, total_ref = refs[n_grad:]
    part, tile = accum_ref.shape

    def weights_of(j, span):
        return high_in[span, :].astype(F32) + low_in[span, :].astype(F32)

    def out(span, j, new, new_row, total):
        high = new.astype(BF16)
        high_ref[span, :] = high
        low_ref[span, :] = (new - high.astype(F32)).astype(BF16)
        new_accum_ref[j : j + 1, :] = new_row
        total_ref[span, :] = total.astype(BF16)

    split_update(tile, part, weights_of, lambda j: accum_ref[j : j + 1, :], grads, out)


def home_update_body(state_ref, accum_ref, total_ref, new_ref, new_accum_ref):
    part, tile = accum_ref.shape

    def out(span, j, new, new_row, total):
        new_ref[span, :] = new
        new_accum_ref[j : j + 1, :] = new_row

    split_update(
        tile, part, lambda j, span: state_ref[span, :], lambda j: accum_ref[j : j + 1, :],
        (total_ref,), out,
    )


def last_update_body(n_grad, side_ref, _, own_ref, sib_ref, own_acc_ref, sib_acc_ref, *refs):
    new_ref, new_accum_ref = refs[-2:]
    part, tile = own_acc_ref.shape
    side = side_ref[0]
    halves = (
        (side, own_ref, own_acc_ref, refs[:n_grad]),
        (1 - side, sib_ref, sib_acc_ref, refs[n_grad : 2 * n_grad]),
    )
    for at, state_ref, accum_ref, grads in halves:

        def out(span, j, new, new_row, total, at=at):
            new_ref[pl.ds(pl.multiple_of((at * part + j) * tile, tile), tile), :] = new
            new_accum_ref[pl.ds(at * part + j, 1), :] = new_row

        split_update(
            tile, part, lambda j, span: state_ref[span, :], lambda j: accum_ref[j : j + 1, :],
            grads, out,
        )


def shifted(value, by):
    count = lax.axis_size("blk")
    return lax.ppermute(value, "blk", [(i, (i + by) % count) for i in range(count)])


def sibling(value):
    return lax.ppermute(value, "grp", [(i, i ^ 1) for i in range(lax.axis_size("grp"))])


def across(value):
    count = lax.axis_size("grp")
    return [
        lax.ppermute(value, "grp", [(i, (i + by) % count) for i in range(count)])
        for by in range(2, count, 2)
    ]


def local(row_factors, row_accum, col_factors, col_accum, tile_values, tile_rows, tile_cols):
    strip_len, width = row_factors.shape
    block_len = col_factors.shape[0]
    _, steps, filled, tile, _ = tile_values.shape
    row_tiles, col_tiles = strip_len // tile, block_len // tile
    half, part = block_len // 2, col_tiles // 2
    side = lax.rem(lax.axis_index("grp"), 2)
    side_arg = jnp.full((1,), side, jnp.int32)
    tr, tc = tile_rows[0], tile_cols[0]
    n_grad = lax.axis_size("grp") // 2
    chunks = 4 if filled % 4 == 0 else 1

    own = sib = col_factors
    accum2 = col_accum.reshape(col_tiles, tile)
    factors, factors_b = row_factors, row_factors
    factor_acc = row_accum.reshape(row_tiles, tile)
    low = own_accum = home = home_accum = None
    pair_flops = 2 * filled * tile * tile * width
    half_f, half_b = shape((half, width), F32), shape((half, width), BF16)
    accum_s = shape((part, tile), F32)
    upd_cost = (8 * half * width, 8 * half * width)

    for step in range(steps):
        last = step == steps - 1
        keep, send, errors = call(
            functools.partial(col_body, step, chunks),
            (half_f, half_b, shape((filled, tile, tile), BF16)),
            [SMEM, SMEM, SMEM, VMEM, VMEM, VMEM, HBM],
            [
                pltpu.VMEM((col_tiles, tile, width), BF16),
                pltpu.VMEM((col_tiles, tile, width), F32),
                pltpu.VMEM((filled, tile, tile), BF16),
                pltpu.VMEM((row_tiles, tile, width), BF16),
                pltpu.SemaphoreType.DMA((chunks,)),
            ],
            2 * pair_flops,
            4 * filled * tile * tile,
        )(side_arg, tr, tc, factors_b, own, sib, tile_values)
        chip_sum = (keep + sibling(send).astype(F32)).astype(BF16)
        moved = shifted(chip_sum, steps - 1) if last and step > 0 else chip_sum
        factors, factor_acc, factors_b = call(
            functools.partial(row_body, step),
            (
                shape((strip_len, width), F32),
                shape((row_tiles, tile), F32),
                shape((strip_len, width), BF16),
            ),
            [SMEM, SMEM, SMEM, VMEM, VMEM, VMEM, VMEM, VMEM, ANY],
            [
                pltpu.VMEM((col_tiles, tile, width), BF16),
                pltpu.VMEM((row_tiles, tile, width), F32),
            ],
            pair_flops,
            10 * strip_len * width,
        )(side_arg, tr, tc, errors, own, sib, factors, factor_acc, chip_sum)
        if last:
            break
        grads = [moved] + across(moved)
        if step == 0:
            high, low, home, home_accum = call(
                functools.partial(first_update_body, n_grad),
                (half_b, half_b, half_f, accum_s),
                [SMEM, ANY] + [VMEM] * (2 + n_grad), [], *upd_cost,
            )(side_arg, factor_acc, col_factors, accum2, *grads)
            own_accum = home_accum
        else:
            high, low, own_accum, total = call(
                functools.partial(next_update_body, n_grad),
                (half_b, half_b, accum_s, half_b),
                [ANY] + [VMEM] * (3 + n_grad), [], *upd_cost,
            )(factor_acc, own, low, own_accum, *grads)
        own = shifted(high, -1)
        low = shifted(low, -1)
        own_accum = shifted(own_accum, -1)
        sib = sibling(own)
        if step > 0:
            home, home_accum = call(
                home_update_body, (half_f, accum_s), [VMEM] * 3, [], *upd_cost
            )(home, home_accum, shifted(total, step))

    if steps == 1:
        home = lax.dynamic_slice_in_dim(col_factors, side * half, half, 0)
        home_accum = lax.dynamic_slice_in_dim(accum2, side * part, part, 0)
    grads = [moved] + across(moved)
    new, new_accum = call(
        functools.partial(last_update_body, n_grad),
        (shape((block_len, width), F32), shape((col_tiles, tile), F32)),
        [SMEM, ANY] + [VMEM] * (4 + 2 * n_grad), [], *upd_cost,
    )(
        side_arg, factor_acc, home, sibling(home), home_accum, sibling(home_accum),
        *grads, *[sibling(g) for g in grads],
    )
    return factors, factor_acc.reshape(strip_len), new, new_accum.reshape(block_len)


def solution(mesh):
    placed = (
        P(("blk", "grp"), None),
        P(("blk", "grp")),
        P("blk", None),
        P("blk"),
        P(("blk", "grp"), None, None, None, None),
        P(("blk", "grp"), None, None),
        P(("blk", "grp"), None, None),
    )
    return jax.shard_map(
        local,
        mesh=mesh,
        in_specs=placed,
        out_specs=(P(("blk", "grp"), None), P(("blk", "grp")), P("blk", None), P("blk")),
        check_vma=False,
    )
```
